32 devices in a mesh: image: 8 (over z, core), dp: 4 (over y, x).
Axes of the slice: x: 2, y: 2, z: 4, core: 2. Of those that a mesh axis runs over, the one named last changes fastest.
Arguments:
- features: bfloat16 [4, 128, 128, 384], P('dp', 'image'), may hold values from -6 to 6
- conv_weight: bfloat16 [3, 3, 128, 128], replicated, may hold values from -0.1875 to 0.1875
- reduce_weight: bfloat16 [256, 128], replicated, may hold values from -0.375 to 0.375
- spectral_weight: bfloat16 [256, 256], replicated, may hold values from -0.375 to 0.375
- expand_weight: bfloat16 [128, 256], replicated, may hold values from -0.5 to 0.5
- upstream: bfloat16 [4, 128, 128, 384], P('dp', 'image'), may hold values from -6 to 6
Outputs:
- feature_grad: bfloat16 [4, 128, 128, 384], P('dp', 'image')
- conv_grad: float32 [3, 3, 128, 128], replicated
- reduce_grad: float32 [256, 128], replicated
- spectral_grad: float32 [256, 256], replicated
- expand_grad: float32 [128, 256], replicated
The draws below stay inside these ranges and needn't reach their ends.
All inputs are finite; a program needn't handle non-finite values.
Results may differ from the reference program's by a relative error of at most 0.014.
Values may be sent and summed in bfloat16 or wider, within the bound.
A program may use at most 64 MiB of HBM per device.

```python
import math
import jax
import jax.numpy as jnp
from jax import lax

H = 128
W = 128
CL = 128
CG = 256
CH = 128
IMAGES = 4


def level_of(stream_key, dims, cuts, least, high):
    def one(position, blocks):
        heights = jax.random.uniform(jax.random.fold_in(jax.random.fold_in(stream_key, 6), position), (blocks,), jnp.float32, least / len(cuts), high / len(cuts))
        return jnp.repeat(jnp.exp(heights), dims[position] // blocks).reshape((-1,) + (1,) * (len(dims) - position - 1))

    loudness = one(*cuts[0])
    for cut in cuts[1:]:
        loudness = loudness * one(*cut)
    return loudness


def scatter_about(stream_key, shape, width, reach, split=(), held_as=jnp.bfloat16):
    values = width * jax.random.normal(stream_key, shape, jnp.float32)
    if split:
        values = values * level_of(stream_key, shape, split, -0.22, 0.18)
    return jnp.clip(values, -reach, reach).astype(held_as)


def setup_inputs(seed: int = 0) -> dict:
    seeds = jax.random.split(jax.random.key(seed), 7)
    features = scatter_about(seeds[0], (IMAGES, H, W, CL + CG), 1.0, 6.0, ((0, 4), (1, 8)))
    conv_weight = scatter_about(seeds[1], (3, 3, CL, CL), (9 * CL) ** -0.5, 0.1875)
    reduce_weight = scatter_about(seeds[2], (CG, CH), CG ** -0.5, 0.375)
    spectral_weight = scatter_about(seeds[3], (2 * CH, 2 * CH), (2 * CH) ** -0.5, 0.375)
    expand_weight = scatter_about(seeds[4], (CH, CG), CH ** -0.5, 0.5)
    upstream = scatter_about(seeds[5], (IMAGES, H, W, CL + CG), 1.0, 6.0, ((0, 4), (1, 8)))
    return {"features": features, "conv_weight": conv_weight, "reduce_weight": reduce_weight, "spectral_weight": spectral_weight, "expand_weight": expand_weight, "upstream": upstream}


def make_tables(length, number):
    lead = lax.broadcasted_iota(jnp.int32, (length, number), 0)
    trail = lax.broadcasted_iota(jnp.int32, (length, number), 1)
    angles = (lead * trail % length).astype(jnp.float32) * (2.0 * math.pi / length)
    factor = 1.0 / math.sqrt(length)
    return ((jnp.cos(angles) * factor).astype(jnp.bfloat16), (-jnp.sin(angles) * factor).astype(jnp.bfloat16))

def inverse_tables(cosine, sine):
    number = cosine.shape[1]
    doubling = jnp.where(lax.broadcasted_iota(jnp.int32, (1, number), 1) == 0, 1.0, 2.0).astype(jnp.bfloat16)
    return ((cosine * doubling).T, (sine * doubling).T)

def product(form, left, right):
    return jnp.einsum(form, left.astype(jnp.float32), right.astype(jnp.float32))

def halves(spectrum):
    half = spectrum.shape[-1] // 2
    return (spectrum[..., :half], spectrum[..., half:])

def height_forward(spectrum, cosine, sine):
    real_part, imag_part = halves(spectrum)
    out_real = product('hm,hkc->mkc', cosine, real_part) - product('hm,hkc->mkc', sine, imag_part)
    out_imag = product('hm,hkc->mkc', cosine, imag_part) + product('hm,hkc->mkc', sine, real_part)
    return jnp.concatenate([out_real, out_imag], axis=-1)

def height_inverse(spectrum, cosine, sine):
    real_part, imag_part = halves(spectrum)
    out_real = product('hm,mkc->hkc', cosine, real_part) + product('hm,mkc->hkc', sine, imag_part)
    out_imag = product('hm,mkc->hkc', cosine, imag_part) - product('hm,mkc->hkc', sine, real_part)
    return jnp.concatenate([out_real, out_imag], axis=-1)

def width_forward(hidden, cosine, sine):
    return jnp.concatenate([product('hwc,wk->hkc', hidden, cosine), product('hwc,wk->hkc', hidden, sine)], axis=-1)

def width_forward_transpose(spectrum, cosine, sine):
    real_part, imag_part = halves(spectrum)
    return product('hkc,wk->hwc', real_part, cosine) + product('hkc,wk->hwc', imag_part, sine)

def width_inverse(spectrum, back_cos, back_sin):
    real_part, imag_part = halves(spectrum)
    return product('hkc,kw->hwc', real_part, back_cos) + product('hkc,kw->hwc', imag_part, back_sin)

def width_inverse_transpose(grad_map, back_cos, back_sin):
    return jnp.concatenate([product('hwc,kw->hkc', grad_map, back_cos), product('hwc,kw->hkc', grad_map, back_sin)], axis=-1)

def silu_slope(values):
    sigma = jax.nn.sigmoid(values)
    return sigma * (1.0 + values * (1.0 - sigma))

def conv_taps(padded, weights, row_count, col_count):
    summed = jnp.zeros((row_count * col_count, weights.shape[3]), jnp.float32)
    for tap_row in range(3):
        for tap_col in range(3):
            window = padded[tap_row:tap_row + row_count, tap_col:tap_col + col_count].reshape(row_count * col_count, -1)
            summed = summed + jnp.dot(window, weights[tap_row, tap_col], preferred_element_type=jnp.float32)
    return summed

def conv_back(padded, weights, row_count, col_count):
    summed = jnp.zeros((row_count * col_count, weights.shape[2]), jnp.float32)
    for tap_row in range(3):
        for tap_col in range(3):
            window = padded[2 - tap_row:2 - tap_row + row_count, 2 - tap_col:2 - tap_col + col_count].reshape(row_count * col_count, -1)
            summed = summed + jnp.dot(window, weights[tap_row, tap_col].T, preferred_element_type=jnp.float32)
    return summed

def conv_grad_terms(padded, grad_flat, row_count, col_count):
    taps = []
    for tap_row in range(3):
        line = []
        for tap_col in range(3):
            window = padded[tap_row:tap_row + row_count, tap_col:tap_col + col_count].reshape(row_count * col_count, -1)
            line.append(product('pi,po->io', window, grad_flat))
        taps.append(jnp.stack(line))
    return jnp.stack(taps)

def single(picture, incoming, conv_weight, reduce_weight, spectral_weight, expand_weight):
    height, breadth, channels = picture.shape
    local_count = conv_weight.shape[2]
    global_count, hidden_count = reduce_weight.shape
    frequencies = breadth // 2
    cos_width, sin_width = make_tables(breadth, frequencies)
    cos_height, sin_height = make_tables(height, height)
    back_cos, back_sin = inverse_tables(cos_width, sin_width)
    x_local = picture[..., :local_count]
    x_global = picture[..., local_count:].reshape(-1, global_count)
    local_pad = jnp.pad(x_local, ((1, 1), (1, 1), (0, 0)))
    y_local = conv_taps(local_pad, conv_weight, height, breadth)
    pre_reduce = jnp.dot(x_global, reduce_weight, preferred_element_type=jnp.float32).reshape(height, breadth, hidden_count)
    hidden = jax.nn.silu(pre_reduce).astype(jnp.bfloat16)
    spectrum = width_forward(hidden, cos_width, sin_width).astype(jnp.bfloat16)
    column_spec = height_forward(spectrum, cos_height, sin_height).astype(jnp.bfloat16)
    flat_spec = column_spec.reshape(-1, 2 * hidden_count)
    pre_mix = jnp.dot(flat_spec, spectral_weight, preferred_element_type=jnp.float32)
    mixture = jax.nn.silu(pre_mix).astype(jnp.bfloat16).reshape(column_spec.shape)
    returned = height_inverse(mixture, cos_height, sin_height).astype(jnp.bfloat16)
    spatial = width_inverse(returned, back_cos, back_sin)
    combined = (hidden.astype(jnp.float32) + spatial).astype(jnp.bfloat16).reshape(-1, hidden_count)
    y_global = jnp.dot(combined, expand_weight, preferred_element_type=jnp.float32)
    y_all = jnp.concatenate([y_local, y_global], axis=-1)
    incoming_flat = incoming.reshape(-1, channels).astype(jnp.float32)
    d_pre = (incoming_flat * silu_slope(y_all)).astype(jnp.bfloat16)
    d_local = d_pre[:, :local_count]
    d_global = d_pre[:, local_count:]
    grad_local = conv_grad_terms(local_pad, d_local, height, breadth)
    d_pad = jnp.pad(d_local.reshape(height, breadth, local_count), ((1, 1), (1, 1), (0, 0)))
    dx_local = conv_back(d_pad, conv_weight, height, breadth)
    d_combined = jnp.dot(d_global, expand_weight.T, preferred_element_type=jnp.float32).astype(jnp.bfloat16)
    grad_expand = product('pi,po->io', combined, d_global)
    d_returned = width_inverse_transpose(d_combined.reshape(height, breadth, hidden_count), back_cos, back_sin).astype(jnp.bfloat16)
    d_mixture = height_forward(d_returned, cos_height, sin_height)
    d_mix = (d_mixture.reshape(-1, 2 * hidden_count) * silu_slope(pre_mix)).astype(jnp.bfloat16)
    grad_spectral = product('pi,po->io', flat_spec, d_mix)
    d_column = jnp.dot(d_mix, spectral_weight.T, preferred_element_type=jnp.float32).astype(jnp.bfloat16).reshape(column_spec.shape)
    d_spectrum = height_inverse(d_column, cos_height, sin_height).astype(jnp.bfloat16)
    d_hidden = d_combined.reshape(height, breadth, hidden_count).astype(jnp.float32) + width_forward_transpose(d_spectrum, cos_width, sin_width)
    d_reduce = (d_hidden * silu_slope(pre_reduce)).astype(jnp.bfloat16).reshape(-1, hidden_count)
    grad_reduce = product('pi,po->io', x_global, d_reduce)
    dx_global = jnp.dot(d_reduce, reduce_weight.T, preferred_element_type=jnp.float32)
    feature_grad = (incoming_flat + jnp.concatenate([dx_local, dx_global], axis=-1)).astype(jnp.bfloat16)
    return (feature_grad.reshape(height, breadth, channels), grad_local, grad_reduce, grad_spectral, grad_expand)

def reference(features, conv_weight, reduce_weight, spectral_weight, expand_weight, upstream):

    def one_image(pair):
        return single(pair[0], pair[1], conv_weight, reduce_weight, spectral_weight, expand_weight)
    feature_grad, grad_local, grad_reduce, grad_spectral, grad_expand = lax.map(one_image, (features, upstream))
    factor = 1.0 / math.sqrt(IMAGES * H * W)
    return (feature_grad, lax.optimization_barrier(jnp.sum(grad_local, axis=0)) * factor, lax.optimization_barrier(jnp.sum(grad_reduce, axis=0)) * factor, lax.optimization_barrier(jnp.sum(grad_spectral, axis=0)) * factor, lax.optimization_barrier(jnp.sum(grad_expand, axis=0)) * factor)
```

```python
import functools
import math

import jax
import jax.numpy as jnp
import numpy as np
from jax import lax
from jax.experimental import pallas as pl
from jax.experimental.pallas import tpu as pltpu
from jax.sharding import PartitionSpec as P

F32 = jnp.float32
BF16 = jnp.bfloat16


def cos_sin(length, number):
    lead = np.arange(length)[:, None]
    trail = np.arange(number)[None, :]
    angles = (lead * trail % length).astype(np.float64) * (2.0 * math.pi / length)
    factor = 1.0 / math.sqrt(length)
    cosine = (np.cos(angles) * factor).astype(np.float32)
    sine = (-np.sin(angles) * factor).astype(np.float32)
    return cosine.astype(BF16), sine.astype(BF16)


def make_tables(breadth, height, groups):
    number = breadth // 2
    owned = number // groups
    cosine, sine = cos_sin(breadth, number)
    both = np.stack([cosine.T, sine.T]).astype(np.float32)
    both = both.reshape(2, groups, owned, breadth).transpose(1, 0, 2, 3).reshape(-1, breadth)
    doubling = np.where(np.arange(number) == 0, 1.0, 2.0).reshape(groups, 1, owned)
    doubling = np.broadcast_to(doubling, (groups, 2, owned)).reshape(-1, 1).astype(np.float32)
    back = both * doubling
    cos_h, sin_h = (t.astype(np.float32) for t in cos_sin(height, height))
    forward = np.block([[cos_h.T, -sin_h.T], [sin_h.T, cos_h.T]])
    inverse = np.block([[cos_h, sin_h], [-sin_h, cos_h]])
    wide = np.stack([both, both.T, back, back.T])
    return jnp.asarray(wide, BF16), jnp.asarray(np.stack([forward, inverse]), BF16)


def dot(left, right, contract=((1,), (0,))):
    return lax.dot_general(left, right, (contract, ((), ())), preferred_element_type=F32)


def slope(values):
    sigma = 1.0 / (1.0 + jnp.exp(-values))
    return sigma * (1.0 + values * (1.0 - sigma))


def silu(values):
    return values / (1.0 + jnp.exp(-values))


def kernel(dims, *refs):
    groups, batch, piece_a, piece_b, factor = dims
    (x_ref, up_ref, wc_ref, wr_ref, ws_ref, we_ref, wide_ref, tall_ref,
     out_ref, gc_ref, gr_ref, gs_ref, ge_ref,
     halo_x, halo_d, x3, d3, wct, pre_red, hidden, comb, dcomb, dglob, dred, scr,
     send1, recv1, send2, recv2, send3, recv3, send4, recv4,
     colspec, premix, dmix, acc_c, acc_r, acc_e, acc_s,
     ga, a_in, a_mid, a_slot, a_quarter, a_full,
     gb, b_slot, b_mid, b_ex, b_full,
     halo_sem, a2a_send, a2a_recv, own_sem, img_send, img_recv, dp_send, dp_recv) = refs
    rows, width, channels = x_ref.shape
    local = wc_ref.shape[1]
    glob, hid = wr_ref.shape
    owned = send1.shape[2]
    spec = width
    height = rows * groups
    me = lax.axis_index("image")
    md = lax.axis_index("dp")

    def img(step):
        return lax.rem(me + step, groups)

    def dpi(step):
        return lax.rem(md + step, batch)

    def remote(src, dst, send_sem, recv_sem, axis, index):
        return pltpu.make_async_remote_copy(
            src_ref=src, dst_ref=dst, send_sem=send_sem, recv_sem=recv_sem,
            device_id={axis: index}, device_id_type=pl.DeviceIdType.MESH)

    barrier = pltpu.get_barrier_semaphore()
    for step in range(1, groups):
        pl.semaphore_signal(barrier, inc=1, device_id={"image": img(step)},
                            device_id_type=pl.DeviceIdType.MESH)
    for step in range(1, batch):
        pl.semaphore_signal(barrier, inc=1, device_id={"dp": dpi(step)},
                            device_id_type=pl.DeviceIdType.MESH)
    pl.semaphore_wait(barrier, groups + batch - 2)

    def halo(source, target, number):
        down = remote(source(rows - 1), target.at[0], halo_sem.at[0, number],
                      halo_sem.at[1, number], "image", img(1))
        up = remote(source(0), target.at[1], halo_sem.at[0, number + 1],
                    halo_sem.at[1, number + 1], "image", img(groups - 1))
        down.start()
        up.start()
        return down, up

    def exchange(source, target, own_source, own_target, number):
        copies = []
        for step in range(1, groups):
            copies.append(remote(source(img(step)), target, a2a_send.at[number, step],
                                 a2a_recv.at[number, step], "image", img(step)))
        for copy in copies:
            copy.start()
        own = pltpu.make_async_copy(own_source, own_target, own_sem.at[number])
        own.start()
        return copies + [own]

    def wait(copies):
        for copy in copies:
            copy.wait()

    def loop(count, unroll=1):
        def run(body):
            lax.fori_loop(0, count, lambda i, c: (body(i), c)[1], 0, unroll=unroll)
        return run

    halo_copies = halo(lambda r: x_ref.at[r, :, pl.ds(0, local)], halo_x, 0)

    @loop(rows, 2)
    def _(h):
        pre = dot(x_ref[h, :, local:], wr_ref[...])
        pre_red[h] = pre
        value = silu(pre).astype(BF16)
        hidden[h] = value
        scr[pl.ds(h, spec, stride=rows), :] = dot(wide_ref[0], value)

    def pack(target):
        @loop(groups)
        def _(g):
            size = 2 * owned * rows
            block = scr[pl.ds(pl.multiple_of(g * size, size), size), :]
            target[g] = block.reshape(2, owned, rows, hid).astype(BF16)

    def unpack(source):
        @loop(groups)
        def _(g):
            size = 2 * owned * rows
            scr[pl.ds(pl.multiple_of(g * size, size), size), :] = (
                source[g].astype(F32).reshape(size, hid))

    pack(send1)
    first = exchange(lambda g: send1.at[g], recv1.at[:, :, me], send1.at[me],
                     recv1.at[:, :, me], 0)

    lane_pos = lax.broadcasted_iota(jnp.int32, (width, local), 0)

    def spread(row, flip):
        row = row.astype(F32)
        before = jnp.where(lane_pos == 0, 0.0, pltpu.roll(row, 1, 0))
        after = jnp.where(lane_pos == width - 1, 0.0, pltpu.roll(row, width - 1, 0))
        parts = (after, row, before) if flip else (before, row, after)
        return jnp.concatenate([p.astype(BF16) for p in parts], axis=1)

    for tap in range(9):
        wct[tap * local:(tap + 1) * local, :] = wc_ref[tap * local:(tap + 1) * local, :].T

    @loop(rows, 2)
    def _(h):
        x3[h + 1] = spread(x_ref[h, :, :local], False)

    wait(halo_copies)
    x3[0] = jnp.where(me > 0, spread(halo_x[0], False), jnp.zeros((), BF16))
    x3[rows + 1] = jnp.where(me < groups - 1, spread(halo_x[1], False), jnp.zeros((), BF16))

    @loop(rows, 2)
    def _(h):
        window = jnp.concatenate([x3[h], x3[h + 1], x3[h + 2]], axis=1)
        y = dot(window, wc_ref[...])
        d = (up_ref[h, :, :local].astype(F32) * slope(y)).astype(BF16)
        d3[h + 1] = spread(d, True)

    halo_copies = halo(lambda r: d3.at[r + 1, :, pl.ds(local, local)], halo_d, 2)

    def column(source, f):
        if rows % 16 == 0:
            real = source[0, f].reshape(height, hid)
            imag = source[1, f].reshape(height, hid)
        else:
            real = source[0, f].astype(F32).reshape(height, hid).astype(BF16)
            imag = source[1, f].astype(F32).reshape(height, hid).astype(BF16)
        return jnp.concatenate([real, imag], axis=0)

    def store(target, f, value):
        for part in range(2):
            half = value[part * height:(part + 1) * height].reshape(groups, rows, hid)
            target[part, f] = half.astype(BF16)

    def across(value):
        return jnp.concatenate([value[:height], value[height:]], axis=1)

    def along(value):
        return jnp.concatenate([value[:, :hid], value[:, hid:]], axis=0)

    wait(first)

    @loop(owned)
    def _(f):
        flat = across(dot(tall_ref[0], column(recv1, f)).astype(BF16))
        colspec[f] = flat
        pre = dot(flat, ws_ref[...])
        premix[f] = pre
        mixture = along(silu(pre).astype(BF16))
        store(send2, f, dot(tall_ref[1], mixture))

    second = exchange(lambda g: send2.at[:, :, g], recv2.at[me], send2.at[:, :, me],
                      recv2.at[me], 1)

    chunk = 4
    acc_c[...] = jnp.zeros_like(acc_c)

    @loop(rows // chunk)
    def _(step):
        h = step * chunk
        turned = d3[pl.ds(h + 1, chunk), :, local:2 * local].reshape(chunk * width, local).T
        for tap in range(3):
            part = x3[pl.ds(h + tap, chunk)].reshape(chunk * width, 3 * local)
            acc_c[tap] += dot(turned, part)

    for a in range(3):
        for b in range(3):
            tap = 3 * a + b
            ga[tap * local:(tap + 1) * local, :] = (
                acc_c[a, :, b * local:(b + 1) * local].T.astype(BF16))

    wait(second)
    unpack(recv2)

    @loop(rows, 2)
    def _(h):
        strip = scr[pl.ds(h, spec, stride=rows), :].astype(BF16)
        value = (hidden[h].astype(F32) + dot(wide_ref[3], strip)).astype(BF16)
        comb[h] = value
        y = dot(value, we_ref[...])
        d = (up_ref[h, :, local:].astype(F32) * slope(y)).astype(BF16)
        dglob[h] = d
        dc = dot(d, we_ref[...], ((1,), (1,))).astype(BF16)
        dcomb[h] = dc
        scr[pl.ds(h, spec, stride=rows), :] = dot(wide_ref[2], dc)

    pack(send3)
    third = exchange(lambda g: send3.at[g], recv3.at[:, :, me], send3.at[me],
                     recv3.at[:, :, me], 2)

    acc_e[...] = jnp.zeros_like(acc_e)

    @loop(rows // chunk)
    def _(step):
        h = step * chunk
        turned = comb[pl.ds(h, chunk)].reshape(chunk * width, hid).T
        acc_e[...] += dot(turned, dglob[pl.ds(h, chunk)].reshape(chunk * width, glob))

    base = 9 * local
    for half in range(glob // hid):
        ga[base + half * hid:base + (half + 1) * hid, :] = (
            acc_e[:, half * hid:(half + 1) * hid].astype(BF16))

    quarter = groups * piece_a

    def part_of(ref, index, size):
        return ref.at[pl.ds(pl.multiple_of(index * size, size), size), :]

    def dp_group(source, target, number):
        copies = []
        for step in range(1, batch):
            copies.append(remote(source(dpi(step)), target(step), dp_send.at[number, step],
                                 dp_recv.at[number, step], "dp", dpi(step)))
        for copy in copies:
            copy.start()
        return copies

    def img_group(source, target, number):
        copies = []
        for step in range(1, groups):
            copies.append(remote(source(img(step)), target(step), img_send.at[number, step],
                                 img_recv.at[number, step], "image", img(step)))
        for copy in copies:
            copy.start()
        return copies

    stage = dp_group(lambda d: part_of(ga, d, quarter), lambda s: a_in.at[s], 0)

    wait(halo_copies)
    d3[0] = jnp.where(me > 0, spread(halo_d[0], True), jnp.zeros((), BF16))
    d3[rows + 1] = jnp.where(me < groups - 1, spread(halo_d[1], True), jnp.zeros((), BF16))

    @loop(rows, 2)
    def _(h):
        window = jnp.concatenate([d3[h + 2], d3[h + 1], d3[h]], axis=1)
        dx = dot(window, wct[...])
        out_ref[h, :, :local] = (up_ref[h, :, :local].astype(F32) + dx).astype(BF16)

    wait(stage)
    total = part_of(ga, md, quarter)[...].astype(F32)
    for step in range(1, batch):
        total += a_in[step].astype(F32)
    a_mid[...] = total.astype(BF16)
    stage = img_group(lambda g: part_of(a_mid, g, piece_a), lambda s: a_slot.at[s], 0)

    wait(third)

    @loop(owned)
    def _(f):
        dm = across(dot(tall_ref[0], column(recv3, f)))
        d = (dm * slope(premix[f])).astype(BF16)
        dmix[f] = d
        dc = along(dot(d, ws_ref[...], ((1,), (1,))).astype(BF16))
        store(send4, f, dot(tall_ref[1], dc))

    fourth = exchange(lambda g: send4.at[:, :, g], recv4.at[me], send4.at[:, :, me],
                      recv4.at[me], 3)

    wait(stage)
    total = part_of(a_mid, me, piece_a)[...].astype(F32)
    for step in range(1, groups):
        total += a_slot[step].astype(F32)
    part_of(a_quarter, me, piece_a)[...] = total.astype(BF16)
    stage = img_group(lambda g: part_of(a_quarter, me, piece_a),
                      lambda s: part_of(a_quarter, me, piece_a), 1)

    acc_s[...] = jnp.zeros_like(acc_s)

    @loop(owned)
    def _(f):
        acc_s[...] += dot(colspec[f].T, dmix[f])

    for half in range(2):
        gb[half * 2 * hid:(half + 1) * 2 * hid, :] = (
            acc_s[:, half * hid:(half + 1) * hid].astype(BF16))

    wait(stage)
    part_of(a_full, md, quarter)[...] = a_quarter[...]
    last = dp_group(lambda d: a_quarter, lambda s: part_of(a_full, md, quarter), 1)

    wait(fourth)
    unpack(recv4)

    @loop(rows, 2)
    def _(h):
        strip = scr[pl.ds(h, spec, stride=rows), :].astype(BF16)
        d = dcomb[h].astype(F32) + dot(wide_ref[1], strip)
        d = (d * slope(pre_red[h])).astype(BF16)
        dred[h] = d

    acc_r[...] = jnp.zeros_like(acc_r)

    @loop(rows // chunk)
    def _(step):
        h = step * chunk
        turned = dred[pl.ds(h, chunk)].reshape(chunk * width, hid).T
        acc_r[...] += dot(turned, x_ref[pl.ds(h, chunk), :, local:].reshape(chunk * width, glob))

    base_r = 4 * hid
    gb[base_r:base_r + glob, :] = acc_r[...].T.astype(BF16)
    stage = img_group(lambda g: part_of(gb, g, piece_b), lambda s: b_slot.at[s], 2)

    @loop(rows, 2)
    def _(h):
        dx = dot(dred[h], wr_ref[...], ((1,), (1,)))
        out_ref[h, :, local:] = (up_ref[h, :, local:].astype(F32) + dx).astype(BF16)

    wait(stage)
    total = part_of(gb, me, piece_b)[...].astype(F32)
    for step in range(1, groups):
        total += b_slot[step].astype(F32)
    b_mid[...] = total.astype(BF16)
    b_ex[md] = b_mid[...]
    stage = dp_group(lambda d: b_mid, lambda s: b_ex.at[md], 2)

    wait(last)
    gc_ref[...] = a_full[:base, :].astype(F32) * factor
    for half in range(glob // hid):
        ge_ref[:, half * hid:(half + 1) * hid] = (
            a_full[base + half * hid:base + (half + 1) * hid, :].astype(F32) * factor)

    wait(stage)
    total = b_ex[0].astype(F32)
    for index in range(1, batch):
        total += b_ex[index].astype(F32)
    part_of(b_full, me, piece_b)[...] = total.astype(BF16)
    stage = img_group(lambda g: part_of(b_full, me, piece_b),
                      lambda s: part_of(b_full, me, piece_b), 3)
    wait(stage)
    for half in range(2):
        gs_ref[:, half * hid:(half + 1) * hid] = (
            b_full[half * 2 * hid:(half + 1) * 2 * hid, :].astype(F32) * factor)
    gr_ref[...] = b_full[base_r:base_r + glob, :].astype(F32) * factor


def round_up(value, unit):
    return -(-value // unit) * unit


def shards(features, conv_weight, reduce_weight, spectral_weight, expand_weight, upstream):
    _, rows, width, channels = features.shape
    local = conv_weight.shape[2]
    glob, hid = reduce_weight.shape
    groups = lax.axis_size("image")
    batch = lax.axis_size("dp")
    height = rows * groups
    owned = width // 2 // groups
    factor = 1.0 / math.sqrt(batch * height * width)
    rows_a = 9 * local + (glob // hid) * hid
    rows_b = 4 * hid + glob
    piece_a = round_up(-(-rows_a // (groups * batch)), 16)
    piece_b = round_up(-(-rows_b // groups), 16)
    wide, tall = make_tables(width, height, groups)

    def vm(*shape, dtype=BF16):
        return pltpu.VMEM(shape, dtype)

    packed = (groups, 2, owned, rows, hid)
    columns = (2, owned, groups, rows, hid)
    dma = pltpu.SemaphoreType.DMA
    scratch = [
        vm(2, width, local), vm(2, width, local),
        vm(rows + 2, width, 3 * local), vm(rows + 2, width, 3 * local),
        vm(9 * local, local),
        vm(rows, width, hid, dtype=F32), vm(rows, width, hid), vm(rows, width, hid),
        vm(rows, width, hid), vm(rows, width, glob), vm(rows, width, hid),
        vm(width * rows, hid, dtype=F32),
        vm(*packed), vm(*columns), vm(*columns), vm(*packed),
        vm(*packed), vm(*columns), vm(*columns), vm(*packed),
        vm(owned, height, 2 * hid), vm(owned, height, 2 * hid, dtype=F32),
        vm(owned, height, 2 * hid),
        vm(3, local, 3 * local, dtype=F32), vm(hid, glob, dtype=F32),
        vm(hid, glob, dtype=F32), vm(2 * hid, 2 * hid, dtype=F32),
        vm(batch * groups * piece_a, hid), vm(batch, groups * piece_a, hid),
        vm(groups * piece_a, hid), vm(groups, piece_a, hid), vm(groups * piece_a, hid),
        vm(batch * groups * piece_a, hid),
        vm(groups * piece_b, hid), vm(groups, piece_b, hid), vm(piece_b, hid),
        vm(batch, piece_b, hid), vm(groups * piece_b, hid),
        dma((2, 4)), dma((4, groups)), dma((4, groups)), dma((4,)),
        dma((4, groups)), dma((4, groups)), dma((3, batch)), dma((3, batch)),
    ]
    outs = (
        jax.ShapeDtypeStruct((rows, width, channels), BF16),
        jax.ShapeDtypeStruct((9 * local, local), F32),
        jax.ShapeDtypeStruct((glob, hid), F32),
        jax.ShapeDtypeStruct((2 * hid, 2 * hid), F32),
        jax.ShapeDtypeStruct((hid, glob), F32),
    )
    space = pl.BlockSpec(memory_space=pltpu.VMEM)
    grad, conv, reduce, spectral, expand = pl.pallas_call(
        functools.partial(kernel, (groups, batch, piece_a, piece_b, factor)),
        out_shape=outs,
        in_specs=[space] * 8,
        out_specs=tuple([space] * 5),
        scratch_shapes=scratch,
        compiler_params=pltpu.CompilerParams(
            collective_id=0, has_side_effects=True, vmem_limit_bytes=56 * 1024 * 1024),
    )(features[0], upstream[0], conv_weight.reshape(9 * local, local), reduce_weight,
      spectral_weight, expand_weight, wide, tall)
    return (grad[None], conv.reshape(conv_weight.shape), reduce, spectral, expand)


def solution(mesh):
    in_specs = (P("dp", "image", None, None), P(), P(), P(), P(), P("dp", "image", None, None))
    out_specs = (P("dp", "image", None, None), P(), P(), P(), P())
    return jax.shard_map(shards, mesh=mesh, in_specs=in_specs, out_specs=out_specs, check_vma=False)
```

```python
import functools
import math

import jax
import jax.numpy as jnp
import numpy as np
from jax import lax
from jax.experimental import pallas as pl
from jax.experimental.pallas import tpu as pltpu
from jax.sharding import PartitionSpec as P

F32 = jnp.float32
BF16 = jnp.bfloat16


def cos_sin(length, number):
    lead = np.arange(length)[:, None]
    trail = np.arange(number)[None, :]
    angles = (lead * trail % length).astype(np.float64) * (2.0 * math.pi / length)
    factor = 1.0 / math.sqrt(length)
    cosine = (np.cos(angles) * factor).astype(np.float32)
    sine = (-np.sin(angles) * factor).astype(np.float32)
    return cosine.astype(BF16), sine.astype(BF16)


def make_tables(breadth, height, groups):
    number = breadth // 2
    owned = number // groups
    cosine, sine = cos_sin(breadth, number)
    both = np.stack([cosine.T, sine.T]).astype(np.float32)
    both = both.reshape(2, groups, owned, breadth).transpose(1, 0, 2, 3).reshape(-1, breadth)
    doubling = np.where(np.arange(number) == 0, 1.0, 2.0).reshape(groups, 1, owned)
    doubling = np.broadcast_to(doubling, (groups, 2, owned)).reshape(-1, 1).astype(np.float32)
    back = both * doubling
    cos_h, sin_h = (t.astype(np.float32) for t in cos_sin(height, height))
    forward = np.block([[cos_h.T, -sin_h.T], [sin_h.T, cos_h.T]])
    inverse = np.block([[cos_h, sin_h], [-sin_h, cos_h]])
    wide = np.stack([both, both.T, back, back.T])
    return jnp.asarray(wide, BF16), jnp.asarray(np.stack([forward, inverse]), BF16)


def dot(left, right, contract=((1,), (0,))):
    return lax.dot_general(left, right, (contract, ((), ())), preferred_element_type=F32)


def slope(values):
    sigma = 1.0 / (1.0 + jnp.exp(-values))
    return sigma * (1.0 + values * (1.0 - sigma))


def silu(values):
    return values / (1.0 + jnp.exp(-values))


def kernel(dims, *refs):
    groups, batch, piece_a, piece_e, piece_b = dims
    (x_ref, up_ref, wc_ref, wr_ref, ws_ref, we_ref, wide_ref, tall_ref,
     out_ref, a_full, e_full, b_full,
     halo_x, halo_d, x3, d3, wct, pre_red, hidden, comb, dcomb, dglob, dred, scr,
     send1, recv1, send2, recv2, send3, recv3, send4, recv4,
     colspec, premix, dmix, acc_c, acc_r, acc_e, acc_s,
     ga, a_in, a_mid, a_slot, a_quarter,
     gx, e_in, e_mid, e_slot, e_quarter,
     gb, b_slot, b_mid, b_ex,
     halo_sem, a2a_send, a2a_recv, own_sem, img_send, img_recv, dp_send, dp_recv) = refs
    rows, width, channels = x_ref.shape
    local = wc_ref.shape[1]
    glob, hid = wr_ref.shape
    owned = send1.shape[2]
    spec = width
    height = rows * groups
    me = lax.axis_index("image")
    md = lax.axis_index("dp")

    def img(step):
        return lax.rem(me + step, groups)

    def dpi(step):
        return lax.rem(md + step, batch)

    def remote(src, dst, send_sem, recv_sem, axis, index):
        return pltpu.make_async_remote_copy(
            src_ref=src, dst_ref=dst, send_sem=send_sem, recv_sem=recv_sem,
            device_id={axis: index}, device_id_type=pl.DeviceIdType.MESH)

    barrier = pltpu.get_barrier_semaphore()
    for step in range(1, groups):
        pl.semaphore_signal(barrier, inc=1, device_id={"image": img(step)},
                            device_id_type=pl.DeviceIdType.MESH)
    for step in range(1, batch):
        pl.semaphore_signal(barrier, inc=1, device_id={"dp": dpi(step)},
                            device_id_type=pl.DeviceIdType.MESH)
    def halo(source, target, number):
        down = remote(source(rows - 1), target.at[0], halo_sem.at[0, number],
                      halo_sem.at[1, number], "image", img(1))
        up = remote(source(0), target.at[1], halo_sem.at[0, number + 1],
                    halo_sem.at[1, number + 1], "image", img(groups - 1))
        down.start()
        up.start()
        return down, up

    parts = 2
    share = owned // parts

    def span(part):
        return pl.ds(part * share, share)

    def exchange(source, target, number):
        copies = []
        for step in range(1, groups):
            copies.append(remote(source(img(step)), target, a2a_send.at[number, step],
                                 a2a_recv.at[number, step], "image", img(step)))
        for copy in copies:
            copy.start()
        own = pltpu.make_async_copy(source(me), target, own_sem.at[number])
        own.start()
        return copies + [own]

    def to_owners(source, target, number):
        return [exchange(lambda g: source.at[g, :, span(part)],
                         target.at[:, span(part), me], number + part) for part in range(parts)]

    def to_strips(source, target, part, number):
        return exchange(lambda g: source.at[:, span(part), g],
                        target.at[me, :, span(part)], number + part)

    def wait(copies):
        for copy in copies:
            copy.wait()

    def loop(count, unroll=1):
        def run(body):
            lax.fori_loop(0, count, lambda i, c: (body(i), c)[1], 0, unroll=unroll)
        return run

    @loop(rows, 4)
    def _(h):
        pre = dot(x_ref[h, :, local:], wr_ref[...])
        pre_red[h] = pre
        value = silu(pre).astype(BF16)
        hidden[h] = value
        scr[pl.ds(h, spec, stride=rows), :] = dot(wide_ref[0], value)

    def pack(target):
        @loop(groups)
        def _(g):
            size = 2 * owned * rows
            block = scr[pl.ds(pl.multiple_of(g * size, size), size), :]
            target[g] = block.reshape(2, owned, rows, hid).astype(BF16)

    def unpack(source):
        @loop(groups)
        def _(g):
            size = 2 * owned * rows
            scr[pl.ds(pl.multiple_of(g * size, size), size), :] = (
                source[g].astype(F32).reshape(size, hid))

    pack(send1)
    pl.semaphore_wait(barrier, groups + batch - 2)
    halo_copies = halo(lambda r: x_ref.at[r, :, pl.ds(0, local)], halo_x, 0)
    first = to_owners(send1, recv1, 0)

    lane_pos = lax.broadcasted_iota(jnp.int32, (width, local), 0)

    def spread(row, flip):
        row = row.astype(F32)
        before = jnp.where(lane_pos == 0, 0.0, pltpu.roll(row, 1, 0))
        after = jnp.where(lane_pos == width - 1, 0.0, pltpu.roll(row, width - 1, 0))
        parts = (after, row, before) if flip else (before, row, after)
        return jnp.concatenate([p.astype(BF16) for p in parts], axis=1)

    for tap in range(9):
        wct[tap * local:(tap + 1) * local, :] = wc_ref[tap * local:(tap + 1) * local, :].T

    @loop(rows, 2)
    def _(h):
        x3[h + 1] = spread(x_ref[h, :, :local], False)

    wait(halo_copies)
    x3[0] = jnp.where(me > 0, spread(halo_x[0], False), jnp.zeros((), BF16))
    x3[rows + 1] = jnp.where(me < groups - 1, spread(halo_x[1], False), jnp.zeros((), BF16))

    @loop(rows, 4)
    def _(h):
        window = jnp.concatenate([x3[h], x3[h + 1], x3[h + 2]], axis=1)
        y = dot(window, wc_ref[...])
        d = (up_ref[h, :, :local].astype(F32) * slope(y)).astype(BF16)
        d3[h + 1] = spread(d, True)

    halo_copies = halo(lambda r: d3.at[r + 1, :, pl.ds(local, local)], halo_d, 2)

    def column(source, f):
        if rows % 16 == 0:
            real = source[0, f].reshape(height, hid)
            imag = source[1, f].reshape(height, hid)
        else:
            real = source[0, f].astype(F32).reshape(height, hid).astype(BF16)
            imag = source[1, f].astype(F32).reshape(height, hid).astype(BF16)
        return jnp.concatenate([real, imag], axis=0)

    def store(target, f, value):
        for part in range(2):
            half = value[part * height:(part + 1) * height].reshape(groups, rows, hid)
            target[part, f] = half.astype(BF16)

    def across(value):
        return jnp.concatenate([value[:height], value[height:]], axis=1)

    def along(value):
        return jnp.concatenate([value[:, :hid], value[:, hid:]], axis=0)

    def forward(part):
        @loop(share, share)
        def _(i):
            f = part * share + i
            flat = across(dot(tall_ref[0], column(recv1, f)).astype(BF16))
            colspec[f] = flat
            pre = dot(flat, ws_ref[...])
            premix[f] = pre
            mixture = along(silu(pre).astype(BF16))
            store(send2, f, dot(tall_ref[1], mixture))

    def part_of(ref, index, size):
        return ref.at[pl.ds(pl.multiple_of(index * size, size), size), :]

    def dp_group(source, target, number):
        copies = []
        for step in range(1, batch):
            copies.append(remote(source(dpi(step)), target(step), dp_send.at[number, step],
                                 dp_recv.at[number, step], "dp", dpi(step)))
        for copy in copies:
            copy.start()
        return copies

    def img_group(source, target, number):
        copies = []
        for step in range(1, groups):
            copies.append(remote(source(img(step)), target(step), img_send.at[number, step],
                                 img_recv.at[number, step], "image", img(step)))
        for copy in copies:
            copy.start()
        return copies

    def sum_one(terms, slots, piece, number):
        size = groups * piece
        return dp_group(lambda d: part_of(terms, d, size), lambda s: slots.at[s], number)

    def sum_two(stage, terms, inbox, mid, slots, piece, number):
        wait(stage)
        total = part_of(terms, md, groups * piece)[...].astype(F32)
        for step in range(1, batch):
            total += inbox[step].astype(F32)
        mid[...] = total.astype(BF16)
        return img_group(lambda g: part_of(mid, g, piece), lambda s: slots.at[s], number)

    def sum_three(stage, mid, slots, quarter, piece, number):
        wait(stage)
        total = part_of(mid, me, piece)[...].astype(F32)
        for step in range(1, groups):
            total += slots[step].astype(F32)
        part_of(quarter, me, piece)[...] = total.astype(BF16)
        return img_group(lambda g: part_of(quarter, me, piece),
                         lambda s: part_of(quarter, me, piece), number)

    def sum_four(stage, quarter, full, piece, number):
        wait(stage)
        size = groups * piece
        part_of(full, md, size)[...] = quarter[...]
        return dp_group(lambda d: quarter, lambda s: part_of(full, md, size), number)

    wait(first[0])
    forward(0)
    second = [to_strips(send2, recv2, 0, 2)]

    chunk = 4
    acc_c[...] = jnp.zeros_like(acc_c)

    @loop(rows // chunk)
    def _(step):
        h = step * chunk
        turned = d3[pl.ds(h + 1, chunk), :, local:2 * local].reshape(chunk * width, local).T
        for tap in range(3):
            part = x3[pl.ds(h + tap, chunk)].reshape(chunk * width, 3 * local)
            acc_c[tap] += dot(turned, part)

    wait(first[1])
    forward(1)
    second.append(to_strips(send2, recv2, 1, 2))

    for a in range(3):
        for b in range(3):
            tap = 3 * a + b
            ga[tap * local:(tap + 1) * local, :] = (
                acc_c[a, :, b * local:(b + 1) * local].T.astype(BF16))

    a_stage = sum_one(ga, a_in, piece_a, 0)

    wait(halo_copies)
    d3[0] = jnp.where(me > 0, spread(halo_d[0], True), jnp.zeros((), BF16))
    d3[rows + 1] = jnp.where(me < groups - 1, spread(halo_d[1], True), jnp.zeros((), BF16))

    @loop(rows, 4)
    def _(h):
        window = jnp.concatenate([d3[h + 2], d3[h + 1], d3[h]], axis=1)
        dx = dot(window, wct[...])
        out_ref[h, :, :local] = (up_ref[h, :, :local].astype(F32) + dx).astype(BF16)

    wait(second[0])
    wait(second[1])
    a_stage = sum_two(a_stage, ga, a_in, a_mid, a_slot, piece_a, 0)
    unpack(recv2)

    @loop(rows, 4)
    def _(h):
        strip = scr[pl.ds(h, spec, stride=rows), :].astype(BF16)
        value = (hidden[h].astype(F32) + dot(wide_ref[3], strip)).astype(BF16)
        comb[h] = value
        y = dot(value, we_ref[...])
        d = (up_ref[h, :, local:].astype(F32) * slope(y)).astype(BF16)
        dglob[h] = d
        dc = dot(d, we_ref[...], ((1,), (1,))).astype(BF16)
        dcomb[h] = dc
        scr[pl.ds(h, spec, stride=rows), :] = dot(wide_ref[2], dc)

    pack(send3)
    third = to_owners(send3, recv3, 4)
    a_stage = sum_three(a_stage, a_mid, a_slot, a_quarter, piece_a, 1)

    acc_e[...] = jnp.zeros_like(acc_e)

    @loop(rows // chunk)
    def _(step):
        h = step * chunk
        turned = comb[pl.ds(h, chunk)].reshape(chunk * width, hid).T
        acc_e[...] += dot(turned, dglob[pl.ds(h, chunk)].reshape(chunk * width, glob))

    for half in range(glob // hid):
        gx[half * hid:(half + 1) * hid, :] = acc_e[:, half * hid:(half + 1) * hid].astype(BF16)

    def backward(part):
        @loop(share, share)
        def _(i):
            f = part * share + i
            dm = across(dot(tall_ref[0], column(recv3, f)))
            d = (dm * slope(premix[f])).astype(BF16)
            dmix[f] = d
            dc = along(dot(d, ws_ref[...], ((1,), (1,))).astype(BF16))
            store(send4, f, dot(tall_ref[1], dc))

    wait(third[0])
    backward(0)
    fourth = [to_strips(send4, recv4, 0, 6)]
    a_stage = sum_four(a_stage, a_quarter, a_full, piece_a, 1)
    wait(third[1])
    backward(1)
    fourth.append(to_strips(send4, recv4, 1, 6))

    acc_s[...] = jnp.zeros_like(acc_s)

    @loop(owned, 4)
    def _(f):
        acc_s[...] += dot(colspec[f].T, dmix[f])

    for half in range(2):
        gx[glob + half * 2 * hid:glob + (half + 1) * 2 * hid, :] = (
            acc_s[:, half * hid:(half + 1) * hid].astype(BF16))

    e_stage = sum_one(gx, e_in, piece_e, 2)
    e_stage = sum_two(e_stage, gx, e_in, e_mid, e_slot, piece_e, 2)

    wait(fourth[0])
    wait(fourth[1])
    unpack(recv4)

    @loop(rows, 4)
    def _(h):
        strip = scr[pl.ds(h, spec, stride=rows), :].astype(BF16)
        d = dcomb[h].astype(F32) + dot(wide_ref[1], strip)
        d = (d * slope(pre_red[h])).astype(BF16)
        dred[h] = d

    e_stage = sum_three(e_stage, e_mid, e_slot, e_quarter, piece_e, 3)
    acc_r[...] = jnp.zeros_like(acc_r)

    @loop(rows // chunk)
    def _(step):
        h = step * chunk
        turned = dred[pl.ds(h, chunk)].reshape(chunk * width, hid).T
        acc_r[...] += dot(turned, x_ref[pl.ds(h, chunk), :, local:].reshape(chunk * width, glob))

    gb[:glob, :] = acc_r[...].T.astype(BF16)
    stage = img_group(lambda g: part_of(gb, g, piece_b), lambda s: b_slot.at[s], 4)
    e_stage = sum_four(e_stage, e_quarter, e_full, piece_e, 3)

    def finish(start):
        @loop(rows // 2, 4)
        def _(i):
            h = start + i
            dx = dot(dred[h], wr_ref[...], ((1,), (1,)))
            out_ref[h, :, local:] = (up_ref[h, :, local:].astype(F32) + dx).astype(BF16)

    finish(0)
    wait(stage)
    total = part_of(gb, me, piece_b)[...].astype(F32)
    for step in range(1, groups):
        total += b_slot[step].astype(F32)
    b_mid[...] = total.astype(BF16)
    b_ex[md] = b_mid[...]
    stage = dp_group(lambda d: b_mid, lambda s: b_ex.at[md], 4)
    finish(rows // 2)
    wait(a_stage)
    wait(stage)
    total = b_ex[0].astype(F32)
    for index in range(1, batch):
        total += b_ex[index].astype(F32)
    part_of(b_full, me, piece_b)[...] = total.astype(BF16)
    stage = img_group(lambda g: part_of(b_full, me, piece_b),
                      lambda s: part_of(b_full, me, piece_b), 5)
    wait(e_stage)
    wait(stage)


def closing(factor, grad_ref, a_ref, e_ref, b_ref, out_ref, gc_ref, gr_ref, gs_ref, ge_ref):
    out_ref[...] = grad_ref[...]
    gc_ref[...] = a_ref[:gc_ref.shape[0], :].astype(F32) * factor
    gr_ref[...] = b_ref[:gr_ref.shape[0], :].astype(F32) * factor
    hid, glob = ge_ref.shape
    for half in range(glob // hid):
        ge_ref[:, half * hid:(half + 1) * hid] = (
            e_ref[half * hid:(half + 1) * hid, :].astype(F32) * factor)
    for half in range(2):
        gs_ref[:, half * hid:(half + 1) * hid] = (
            e_ref[glob + half * 2 * hid:glob + (half + 1) * 2 * hid, :].astype(F32) * factor)


def round_up(value, unit):
    return -(-value // unit) * unit


def shards(features, conv_weight, reduce_weight, spectral_weight, expand_weight, upstream):
    _, rows, width, channels = features.shape
    local = conv_weight.shape[2]
    glob, hid = reduce_weight.shape
    groups = lax.axis_size("image")
    batch = lax.axis_size("dp")
    height = rows * groups
    owned = width // 2 // groups
    factor = 1.0 / math.sqrt(batch * height * width)
    rows_a = 9 * local
    rows_e = glob + 4 * hid
    rows_b = glob
    piece_a = round_up(-(-rows_a // (groups * batch)), 16)
    piece_e = round_up(-(-rows_e // (groups * batch)), 16)
    piece_b = round_up(-(-rows_b // groups), 16)
    wide, tall = make_tables(width, height, groups)

    def vm(*shape, dtype=BF16):
        return pltpu.VMEM(shape, dtype)

    packed = (groups, 2, owned, rows, hid)
    columns = (2, owned, groups, rows, hid)
    dma = pltpu.SemaphoreType.DMA
    scratch = [
        vm(2, width, local), vm(2, width, local),
        vm(rows + 2, width, 3 * local), vm(rows + 2, width, 3 * local),
        vm(9 * local, local),
        vm(rows, width, hid, dtype=F32), vm(rows, width, hid), vm(rows, width, hid),
        vm(rows, width, hid), vm(rows, width, glob), vm(rows, width, hid),
        vm(width * rows, hid, dtype=F32),
        vm(*packed), vm(*columns), vm(*columns), vm(*packed),
        vm(*packed), vm(*columns), vm(*columns), vm(*packed),
        vm(owned, height, 2 * hid), vm(owned, height, 2 * hid, dtype=F32),
        vm(owned, height, 2 * hid),
        vm(3, local, 3 * local, dtype=F32), vm(hid, glob, dtype=F32),
        vm(hid, glob, dtype=F32), vm(2 * hid, 2 * hid, dtype=F32),
        vm(batch * groups * piece_a, hid), vm(batch, groups * piece_a, hid),
        vm(groups * piece_a, hid), vm(groups, piece_a, hid), vm(groups * piece_a, hid),
        vm(batch * groups * piece_e, hid), vm(batch, groups * piece_e, hid),
        vm(groups * piece_e, hid), vm(groups, piece_e, hid), vm(groups * piece_e, hid),
        vm(groups * piece_b, hid), vm(groups, piece_b, hid), vm(piece_b, hid),
        vm(batch, piece_b, hid),
        dma((2, 4)), dma((8, groups)), dma((8, groups)), dma((8,)),
        dma((6, groups)), dma((6, groups)), dma((5, batch)), dma((5, batch)),
    ]
    outs = (
        jax.ShapeDtypeStruct((rows, width, channels), BF16),
        jax.ShapeDtypeStruct((batch * groups * piece_a, hid), BF16),
        jax.ShapeDtypeStruct((batch * groups * piece_e, hid), BF16),
        jax.ShapeDtypeStruct((groups * piece_b, hid), BF16),
    )
    results = (
        jax.ShapeDtypeStruct((rows, width, channels), BF16),
        jax.ShapeDtypeStruct((9 * local, local), F32),
        jax.ShapeDtypeStruct((glob, hid), F32),
        jax.ShapeDtypeStruct((2 * hid, 2 * hid), F32),
        jax.ShapeDtypeStruct((hid, glob), F32),
    )
    space = pl.BlockSpec(memory_space=pltpu.VMEM)
    partial = pl.pallas_call(
        functools.partial(kernel, (groups, batch, piece_a, piece_e, piece_b)),
        out_shape=outs,
        in_specs=[space] * 8,
        out_specs=tuple([space] * 4),
        scratch_shapes=scratch,
        compiler_params=pltpu.CompilerParams(
            collective_id=0, has_side_effects=True, vmem_limit_bytes=40 * 1024 * 1024),
    )(features[0], upstream[0], conv_weight.reshape(9 * local, local), reduce_weight,
      spectral_weight, expand_weight, wide, tall)
    grad, conv, reduce, spectral, expand = pl.pallas_call(
        functools.partial(closing, factor),
        out_shape=results,
        in_specs=[space] * 4,
        out_specs=tuple([space] * 5),
        compiler_params=pltpu.CompilerParams(vmem_limit_bytes=16 * 1024 * 1024),
    )(*partial)
    return (grad[None], conv.reshape(conv_weight.shape), reduce, spectral, expand)


def solution(mesh):
    in_specs = (P("dp", "image", None, None), P(), P(), P(), P(), P("dp", "image", None, None))
    out_specs = (P("dp", "image", None, None), P(), P(), P(), P())
    return jax.shard_map(shards, mesh=mesh, in_specs=in_specs, out_specs=out_specs, check_vma=False)
```

```python
import functools
import math

import jax
import jax.numpy as jnp
import numpy as np
from jax import lax
from jax.experimental import pallas as pl
from jax.experimental.pallas import tpu as pltpu
from jax.sharding import PartitionSpec as P

F32 = jnp.float32
BF16 = jnp.bfloat16


def cos_sin(length, number):
    lead = np.arange(length)[:, None]
    trail = np.arange(number)[None, :]
    angles = (lead * trail % length).astype(np.float64) * (2.0 * math.pi / length)
    factor = 1.0 / math.sqrt(length)
    cosine = (np.cos(angles) * factor).astype(np.float32)
    sine = (-np.sin(angles) * factor).astype(np.float32)
    return cosine.astype(BF16), sine.astype(BF16)


def make_tables(breadth, height, groups):
    number = breadth // 2
    owned = number // groups
    cosine, sine = cos_sin(breadth, number)
    both = np.stack([cosine.T, sine.T]).astype(np.float32)
    both = both.reshape(2, groups, owned, breadth).transpose(1, 0, 2, 3).reshape(-1, breadth)
    doubling = np.where(np.arange(number) == 0, 1.0, 2.0).reshape(groups, 1, owned)
    doubling = np.broadcast_to(doubling, (groups, 2, owned)).reshape(-1, 1).astype(np.float32)
    back = both * doubling
    cos_h, sin_h = (t.astype(np.float32) for t in cos_sin(height, height))
    forward = np.block([[cos_h.T, -sin_h.T], [sin_h.T, cos_h.T]])
    inverse = np.block([[cos_h, sin_h], [-sin_h, cos_h]])
    wide = np.stack([both, both.T, back, back.T])
    return jnp.asarray(wide, BF16), jnp.asarray(np.stack([forward, inverse]), BF16)


def dot(left, right, contract=((1,), (0,))):
    return lax.dot_general(left, right, (contract, ((), ())), preferred_element_type=F32)


def slope(values):
    sigma = 0.5 + 0.5 * jnp.tanh(0.5 * values)
    return sigma * (1.0 + values * (1.0 - sigma))


def silu(values):
    return values * (0.5 + 0.5 * jnp.tanh(0.5 * values))


def kernel(dims, *refs):
    groups, batch, piece_a, piece_e, piece_b = dims
    operands, refs = refs[:8], refs[8:]
    (out_ref, a_full, e_full, b_full,
     x_ref, up_ref, wc_ref, wr_ref, ws_ref, we_ref, wide_ref, tall_ref, load_sem,
     halo_x, halo_d, x3, d3, wct, pre_red, hidden, comb, dcomb, dglob, dred, scr,
     send1, recv1, send2, recv2, send3, recv3, send4, recv4,
     colspec, premix, dmix, acc_c, acc_r, acc_e, acc_s,
     ga, a_in, a_mid, a_slot, a_quarter,
     gx, e_in, e_mid, e_slot, e_quarter,
     gb, b_slot, b_mid, b_ex,
     halo_sem, a2a_send, a2a_recv, own_sem, img_send, img_recv, dp_send, dp_recv) = refs
    rows, width, channels = x_ref.shape
    local = wc_ref.shape[1]
    glob, hid = wr_ref.shape
    owned = send1.shape[2]
    spec = width
    height = rows * groups
    me = lax.axis_index("image")
    md = lax.axis_index("dp")

    def img(step):
        return lax.rem(me + step, groups)

    def dpi(step):
        return lax.rem(md + step, batch)

    def remote(src, dst, send_sem, recv_sem, axis, index):
        return pltpu.make_async_remote_copy(
            src_ref=src, dst_ref=dst, send_sem=send_sem, recv_sem=recv_sem,
            device_id={axis: index}, device_id_type=pl.DeviceIdType.MESH)

    staged = (x_ref, up_ref, wc_ref, wr_ref, ws_ref, we_ref, wide_ref, tall_ref)
    loads = [pltpu.make_async_copy(operands[i], staged[i], load_sem.at[i]) for i in range(8)]
    early, late = (0, 3, 6), (2, 1, 7, 4, 5)
    for i in early + late:
        loads[i].start()

    barrier = pltpu.get_barrier_semaphore()
    for step in range(1, groups):
        pl.semaphore_signal(barrier, inc=1, device_id={"image": img(step)},
                            device_id_type=pl.DeviceIdType.MESH)
    for step in range(1, batch):
        pl.semaphore_signal(barrier, inc=1, device_id={"dp": dpi(step)},
                            device_id_type=pl.DeviceIdType.MESH)
    def halo(source, target, number):
        down = remote(source(rows - 1), target.at[0], halo_sem.at[0, number],
                      halo_sem.at[1, number], "image", img(1))
        up = remote(source(0), target.at[1], halo_sem.at[0, number + 1],
                    halo_sem.at[1, number + 1], "image", img(groups - 1))
        down.start()
        up.start()
        return down, up

    parts = 2
    share = owned // parts

    def span(part):
        return pl.ds(part * share, share)

    def exchange(source, target, number):
        copies = []
        for step in range(1, groups):
            copies.append(remote(source(img(step)), target, a2a_send.at[number, step],
                                 a2a_recv.at[number, step], "image", img(step)))
        for copy in copies:
            copy.start()
        own = pltpu.make_async_copy(source(me), target, own_sem.at[number])
        own.start()
        return copies + [own]

    def to_owners(source, target, number):
        return [exchange(lambda g: source.at[g, :, span(part)],
                         target.at[:, span(part), me], number + part) for part in range(parts)]

    def to_strips(source, target, part, number):
        return exchange(lambda g: source.at[:, span(part), g],
                        target.at[me, :, span(part)], number + part)

    def wait(copies):
        for copy in copies:
            copy.wait()

    def loop(count, unroll=1):
        def run(body):
            lax.fori_loop(0, count, lambda i, c: (body(i), c)[1], 0, unroll=unroll)
        return run

    wait(loads[i] for i in early)

    @loop(rows, 4)
    def _(h):
        pre = dot(x_ref[h, :, local:], wr_ref[...])
        pre_red[h] = pre
        value = silu(pre).astype(BF16)
        hidden[h] = value
        scr[pl.ds(h, spec, stride=rows), :] = dot(wide_ref[0], value)

    def pack(target):
        @loop(groups)
        def _(g):
            size = 2 * owned * rows
            block = scr[pl.ds(pl.multiple_of(g * size, size), size), :]
            target[g] = block.reshape(2, owned, rows, hid).astype(BF16)

    def unpack(source):
        @loop(groups)
        def _(g):
            size = 2 * owned * rows
            scr[pl.ds(pl.multiple_of(g * size, size), size), :] = (
                source[g].astype(F32).reshape(size, hid))

    pack(send1)
    pl.semaphore_wait(barrier, groups + batch - 2)
    halo_copies = halo(lambda r: x_ref.at[r, :, pl.ds(0, local)], halo_x, 0)
    first = to_owners(send1, recv1, 0)
    wait(loads[i] for i in late)

    lane_pos = lax.broadcasted_iota(jnp.int32, (width, local), 0)

    def spread(row, flip):
        row = row.astype(F32)
        before = jnp.where(lane_pos == 0, 0.0, pltpu.roll(row, 1, 0))
        after = jnp.where(lane_pos == width - 1, 0.0, pltpu.roll(row, width - 1, 0))
        parts = (after, row, before) if flip else (before, row, after)
        return jnp.concatenate([p.astype(BF16) for p in parts], axis=1)

    for tap in range(9):
        wct[tap * local:(tap + 1) * local, :] = wc_ref[tap * local:(tap + 1) * local, :].T

    @loop(rows, 2)
    def _(h):
        x3[h + 1] = spread(x_ref[h, :, :local], False)

    wait(halo_copies)
    x3[0] = jnp.where(me > 0, spread(halo_x[0], False), jnp.zeros((), BF16))
    x3[rows + 1] = jnp.where(me < groups - 1, spread(halo_x[1], False), jnp.zeros((), BF16))

    @loop(rows, 4)
    def _(h):
        window = jnp.concatenate([x3[h], x3[h + 1], x3[h + 2]], axis=1)
        y = dot(window, wc_ref[...])
        d = (up_ref[h, :, :local].astype(F32) * slope(y)).astype(BF16)
        d3[h + 1] = spread(d, True)

    halo_copies = halo(lambda r: d3.at[r + 1, :, pl.ds(local, local)], halo_d, 2)

    def column(source, f):
        if rows % 16 == 0:
            real = source[0, f].reshape(height, hid)
            imag = source[1, f].reshape(height, hid)
        else:
            real = source[0, f].astype(F32).reshape(height, hid).astype(BF16)
            imag = source[1, f].astype(F32).reshape(height, hid).astype(BF16)
        return jnp.concatenate([real, imag], axis=0)

    def store(target, f, value):
        for part in range(2):
            half = value[part * height:(part + 1) * height].reshape(groups, rows, hid)
            target[part, f] = half.astype(BF16)

    def across(value):
        return jnp.concatenate([value[:height], value[height:]], axis=1)

    def along(value):
        return jnp.concatenate([value[:, :hid], value[:, hid:]], axis=0)

    def forward(part):
        @loop(share, share)
        def _(i):
            f = part * share + i
            flat = across(dot(tall_ref[0], column(recv1, f)).astype(BF16))
            colspec[f] = flat
            pre = dot(flat, ws_ref[...])
            premix[f] = pre
            mixture = along(silu(pre).astype(BF16))
            store(send2, f, dot(tall_ref[1], mixture))

    def part_of(ref, index, size):
        return ref.at[pl.ds(pl.multiple_of(index * size, size), size), :]

    def dp_group(source, target, number):
        copies = []
        for step in range(1, batch):
            copies.append(remote(source(dpi(step)), target(step), dp_send.at[number, step],
                                 dp_recv.at[number, step], "dp", dpi(step)))
        for copy in copies:
            copy.start()
        return copies

    def img_group(source, target, number):
        copies = []
        for step in range(1, groups):
            copies.append(remote(source(img(step)), target(step), img_send.at[number, step],
                                 img_recv.at[number, step], "image", img(step)))
        for copy in copies:
            copy.start()
        return copies

    def sum_one(terms, slots, piece, number):
        size = groups * piece
        return dp_group(lambda d: part_of(terms, d, size), lambda s: slots.at[s], number)

    def sum_two(stage, terms, inbox, mid, slots, piece, number):
        wait(stage)
        total = part_of(terms, md, groups * piece)[...].astype(F32)
        for step in range(1, batch):
            total += inbox[step].astype(F32)
        mid[...] = total.astype(BF16)
        return img_group(lambda g: part_of(mid, g, piece), lambda s: slots.at[s], number)

    def sum_three(stage, mid, slots, quarter, piece, number):
        wait(stage)
        total = part_of(mid, me, piece)[...].astype(F32)
        for step in range(1, groups):
            total += slots[step].astype(F32)
        part_of(quarter, me, piece)[...] = total.astype(BF16)
        return img_group(lambda g: part_of(quarter, me, piece),
                         lambda s: part_of(quarter, me, piece), number)

    def sum_four(stage, quarter, full, piece, number):
        wait(stage)
        size = groups * piece
        part_of(full, md, size)[...] = quarter[...]
        return dp_group(lambda d: quarter, lambda s: part_of(full, md, size), number)

    wait(first[0])
    forward(0)
    second = [to_strips(send2, recv2, 0, 2)]

    chunk = 4
    acc_c[...] = jnp.zeros_like(acc_c)

    @loop(rows // chunk)
    def _(step):
        h = step * chunk
        turned = d3[pl.ds(h + 1, chunk), :, local:2 * local].reshape(chunk * width, local).T
        for tap in range(3):
            part = x3[pl.ds(h + tap, chunk)].reshape(chunk * width, 3 * local)
            acc_c[tap] += dot(turned, part)

    wait(first[1])
    forward(1)
    second.append(to_strips(send2, recv2, 1, 2))

    for a in range(3):
        for b in range(3):
            tap = 3 * a + b
            ga[tap * local:(tap + 1) * local, :] = (
                acc_c[a, :, b * local:(b + 1) * local].T.astype(BF16))

    a_stage = sum_one(ga, a_in, piece_a, 0)

    wait(halo_copies)
    d3[0] = jnp.where(me > 0, spread(halo_d[0], True), jnp.zeros((), BF16))
    d3[rows + 1] = jnp.where(me < groups - 1, spread(halo_d[1], True), jnp.zeros((), BF16))

    @loop(rows, 4)
    def _(h):
        window = jnp.concatenate([d3[h + 2], d3[h + 1], d3[h]], axis=1)
        dx = dot(window, wct[...])
        out_ref[h, :, :local] = (up_ref[h, :, :local].astype(F32) + dx).astype(BF16)

    wait(second[0])
    wait(second[1])
    a_stage = sum_two(a_stage, ga, a_in, a_mid, a_slot, piece_a, 0)
    unpack(recv2)

    def expand(i):
        h = i
        strip = scr[pl.ds(h, spec, stride=rows), :].astype(BF16)
        value = (hidden[h].astype(F32) + dot(wide_ref[3], strip)).astype(BF16)
        comb[h] = value
        y = dot(value, we_ref[...])
        d = (up_ref[h, :, local:].astype(F32) * slope(y)).astype(BF16)
        dglob[h] = d
        dc = dot(d, we_ref[...], ((1,), (1,))).astype(BF16)
        dcomb[h] = dc
        scr[pl.ds(h, spec, stride=rows), :] = dot(wide_ref[2], dc)

    loop(rows // 2, 4)(expand)
    a_stage = sum_three(a_stage, a_mid, a_slot, a_quarter, piece_a, 1)
    loop(rows // 2, 4)(lambda i: expand(i + rows // 2))
    pack(send3)
    third = to_owners(send3, recv3, 4)

    acc_e[...] = jnp.zeros_like(acc_e)

    @loop(rows // chunk)
    def _(step):
        h = step * chunk
        turned = comb[pl.ds(h, chunk)].reshape(chunk * width, hid).T
        acc_e[...] += dot(turned, dglob[pl.ds(h, chunk)].reshape(chunk * width, glob))

    for half in range(glob // hid):
        gx[half * hid:(half + 1) * hid, :] = acc_e[:, half * hid:(half + 1) * hid].astype(BF16)

    def backward(part):
        @loop(share, share)
        def _(i):
            f = part * share + i
            dm = across(dot(tall_ref[0], column(recv3, f)))
            d = (dm * slope(premix[f])).astype(BF16)
            dmix[f] = d
            dc = along(dot(d, ws_ref[...], ((1,), (1,))).astype(BF16))
            store(send4, f, dot(tall_ref[1], dc))

    wait(third[0])
    backward(0)
    fourth = [to_strips(send4, recv4, 0, 6)]
    a_stage = sum_four(a_stage, a_quarter, a_full, piece_a, 1)
    wait(third[1])
    backward(1)
    fourth.append(to_strips(send4, recv4, 1, 6))

    acc_s[...] = jnp.zeros_like(acc_s)

    @loop(owned, 4)
    def _(f):
        acc_s[...] += dot(colspec[f].T, dmix[f])

    for half in range(2):
        gx[glob + half * 2 * hid:glob + (half + 1) * 2 * hid, :] = (
            acc_s[:, half * hid:(half + 1) * hid].astype(BF16))

    e_stage = sum_one(gx, e_in, piece_e, 2)
    wait(fourth[0])
    wait(fourth[1])
    e_stage = sum_two(e_stage, gx, e_in, e_mid, e_slot, piece_e, 2)
    unpack(recv4)

    @loop(rows, 4)
    def _(h):
        strip = scr[pl.ds(h, spec, stride=rows), :].astype(BF16)
        d = dcomb[h].astype(F32) + dot(wide_ref[1], strip)
        d = (d * slope(pre_red[h])).astype(BF16)
        dred[h] = d

    e_stage = sum_three(e_stage, e_mid, e_slot, e_quarter, piece_e, 3)
    acc_r[...] = jnp.zeros_like(acc_r)

    @loop(rows // chunk)
    def _(step):
        h = step * chunk
        turned = dred[pl.ds(h, chunk)].reshape(chunk * width, hid).T
        acc_r[...] += dot(turned, x_ref[pl.ds(h, chunk), :, local:].reshape(chunk * width, glob))

    gb[:glob, :] = acc_r[...].T.astype(BF16)
    stage = img_group(lambda g: part_of(gb, g, piece_b), lambda s: b_slot.at[s], 4)
    e_stage = sum_four(e_stage, e_quarter, e_full, piece_e, 3)

    def finish(start):
        @loop(rows // 2, 4)
        def _(i):
            h = start + i
            dx = dot(dred[h], wr_ref[...], ((1,), (1,)))
            out_ref[h, :, local:] = (up_ref[h, :, local:].astype(F32) + dx).astype(BF16)

    finish(0)
    wait(stage)
    total = part_of(gb, me, piece_b)[...].astype(F32)
    for step in range(1, groups):
        total += b_slot[step].astype(F32)
    b_mid[...] = total.astype(BF16)
    b_ex[md] = b_mid[...]
    stage = dp_group(lambda d: b_mid, lambda s: b_ex.at[md], 4)
    finish(rows // 2)
    wait(a_stage)
    wait(stage)
    total = b_ex[0].astype(F32)
    for index in range(1, batch):
        total += b_ex[index].astype(F32)
    part_of(b_full, me, piece_b)[...] = total.astype(BF16)
    stage = img_group(lambda g: part_of(b_full, me, piece_b),
                      lambda s: part_of(b_full, me, piece_b), 5)
    wait(e_stage)
    wait(stage)


def closing(factor, grad_ref, a_ref, e_ref, b_ref, out_ref, gc_ref, gr_ref, gs_ref, ge_ref):
    out_ref[...] = grad_ref[...]
    gc_ref[...] = a_ref[:gc_ref.shape[0], :].astype(F32) * factor
    gr_ref[...] = b_ref[:gr_ref.shape[0], :].astype(F32) * factor
    hid, glob = ge_ref.shape
    for half in range(glob // hid):
        ge_ref[:, half * hid:(half + 1) * hid] = (
            e_ref[half * hid:(half + 1) * hid, :].astype(F32) * factor)
    for half in range(2):
        gs_ref[:, half * hid:(half + 1) * hid] = (
            e_ref[glob + half * 2 * hid:glob + (half + 1) * 2 * hid, :].astype(F32) * factor)


def round_up(value, unit):
    return -(-value // unit) * unit


def shards(features, conv_weight, reduce_weight, spectral_weight, expand_weight, upstream):
    _, rows, width, channels = features.shape
    local = conv_weight.shape[2]
    glob, hid = reduce_weight.shape
    groups = lax.axis_size("image")
    batch = lax.axis_size("dp")
    height = rows * groups
    owned = width // 2 // groups
    factor = 1.0 / math.sqrt(batch * height * width)
    rows_a = 9 * local
    rows_e = glob + 4 * hid
    rows_b = glob
    piece_a = round_up(-(-rows_a // (groups * batch)), 16)
    piece_e = round_up(-(-rows_e // (groups * batch)), 16)
    piece_b = round_up(-(-rows_b // groups), 16)
    wide, tall = make_tables(width, height, groups)

    def vm(*shape, dtype=BF16):
        return pltpu.VMEM(shape, dtype)

    packed = (groups, 2, owned, rows, hid)
    columns = (2, owned, groups, rows, hid)
    dma = pltpu.SemaphoreType.DMA
    operands = (features[0], upstream[0], conv_weight.reshape(9 * local, local), reduce_weight,
                spectral_weight, expand_weight, wide, tall)
    scratch = [pltpu.VMEM(v.shape, v.dtype) for v in operands] + [dma((8,))]
    scratch += [
        vm(2, width, local), vm(2, width, local),
        vm(rows + 2, width, 3 * local), vm(rows + 2, width, 3 * local),
        vm(9 * local, local),
        vm(rows, width, hid, dtype=F32), vm(rows, width, hid), vm(rows, width, hid),
        vm(rows, width, hid), vm(rows, width, glob), vm(rows, width, hid),
        vm(width * rows, hid, dtype=F32),
        vm(*packed), vm(*columns), vm(*columns), vm(*packed),
        vm(*packed), vm(*columns), vm(*columns), vm(*packed),
        vm(owned, height, 2 * hid), vm(owned, height, 2 * hid, dtype=F32),
        vm(owned, height, 2 * hid),
        vm(3, local, 3 * local, dtype=F32), vm(hid, glob, dtype=F32),
        vm(hid, glob, dtype=F32), vm(2 * hid, 2 * hid, dtype=F32),
        vm(batch * groups * piece_a, hid), vm(batch, groups * piece_a, hid),
        vm(groups * piece_a, hid), vm(groups, piece_a, hid), vm(groups * piece_a, hid),
        vm(batch * groups * piece_e, hid), vm(batch, groups * piece_e, hid),
        vm(groups * piece_e, hid), vm(groups, piece_e, hid), vm(groups * piece_e, hid),
        vm(groups * piece_b, hid), vm(groups, piece_b, hid), vm(piece_b, hid),
        vm(batch, piece_b, hid),
        dma((2, 4)), dma((8, groups)), dma((8, groups)), dma((8,)),
        dma((6, groups)), dma((6, groups)), dma((5, batch)), dma((5, batch)),
    ]
    outs = (
        jax.ShapeDtypeStruct((rows, width, channels), BF16),
        jax.ShapeDtypeStruct((batch * groups * piece_a, hid), BF16),
        jax.ShapeDtypeStruct((batch * groups * piece_e, hid), BF16),
        jax.ShapeDtypeStruct((groups * piece_b, hid), BF16),
    )
    results = (
        jax.ShapeDtypeStruct((rows, width, channels), BF16),
        jax.ShapeDtypeStruct((9 * local, local), F32),
        jax.ShapeDtypeStruct((glob, hid), F32),
        jax.ShapeDtypeStruct((2 * hid, 2 * hid), F32),
        jax.ShapeDtypeStruct((hid, glob), F32),
    )
    space = pl.BlockSpec(memory_space=pltpu.VMEM)
    partial = pl.pallas_call(
        functools.partial(kernel, (groups, batch, piece_a, piece_e, piece_b)),
        out_shape=outs,
        in_specs=[pl.BlockSpec(memory_space=pltpu.HBM)] * 8,
        out_specs=tuple([space] * 4),
        scratch_shapes=scratch,
        compiler_params=pltpu.CompilerParams(
            collective_id=0, has_side_effects=True, vmem_limit_bytes=40 * 1024 * 1024),
    )(*[pltpu.with_memory_space_constraint(v, pltpu.HBM) for v in operands])
    grad, conv, reduce, spectral, expand = pl.pallas_call(
        functools.partial(closing, factor),
        out_shape=results,
        in_specs=[space] * 4,
        out_specs=tuple([space] * 5),
        compiler_params=pltpu.CompilerParams(vmem_limit_bytes=16 * 1024 * 1024),
    )(*partial)
    return (grad[None], conv.reshape(conv_weight.shape), reduce, spectral, expand)


def solution(mesh):
    in_specs = (P("dp", "image", None, None), P(), P(), P(), P(), P("dp", "image", None, None))
    out_specs = (P("dp", "image", None, None), P(), P(), P(), P())
    return jax.shard_map(shards, mesh=mesh, in_specs=in_specs, out_specs=out_specs, check_vma=False)
```
